1024 devices in a mesh: dp: 16 (over x, y), expert: 64 (over z, core).
Axes of the slice: x: 4, y: 4, z: 32, core: 2. Of those that a mesh axis runs over, the one named last changes fastest.
Arguments:
- tokens: bfloat16 [131072, 2048], P(('dp', 'expert')), may hold values from -24 to 24
- upstream: bfloat16 [131072, 2048], P(('dp', 'expert')), may hold values from -6 to 6
- w_up: bfloat16 [64, 2048, 768], P('expert'), may hold values from -0.125 to 0.125
- w_down: bfloat16 [64, 2048, 768], P('expert'), may hold values from -0.21875 to 0.21875
- routes: int32 [131072, 1], P(('dp', 'expert')), may hold values from 0 to 63; in each aligned block of 128 rows (0 to 127, 128 to 255, ...) at most 3 rows name the same one
- gate_share: int32 [131072, 1], P(('dp', 'expert')), may hold values from 1 to 256
Outputs:
- token_grad: bfloat16 [131072, 2048], P(('dp', 'expert'))
- gate_grad: bfloat16 [131072, 1], P(('dp', 'expert'))
- up_grad: float32 [64, 2048, 768], P('expert', 'dp')
- down_grad: float32 [64, 2048, 768], P('expert', 'dp')
The draws below stay inside these ranges and needn't reach their ends.
Inputs may be any that keep to these rules, and one draw needn't show every extreme that they name: `routes`: within the 128 tokens of one device each expert is named by at most 3 rows, and by exactly 3 for some expert.
All inputs are finite; a program needn't handle non-finite values.
Results may differ from the reference program's by a relative error of at most 0.013.
Values may be sent and summed in bfloat16 or wider, within the bound.
No kernel may reach another device: no remote copies, remote signals or barrier semaphores. Data moves between devices by JAX's collectives and lax.ppermute only.
A program may use at most 64 MiB of HBM per device.

```python
import math
import jax
import jax.numpy as jnp
import numpy as np
from jax import lax

D = 2048
F = 768
TOPK = 1
GATE_DEN = 256
TOK_DEV = 128
EXPERTS = 64
CAP = 3
TOKENS = 131072
N_DP = 16
N_EXPERT = 64


def touch_ends(entries, stream_key, smallest, high):
    dims = entries.shape
    place = [jax.random.randint(jax.random.fold_in(stream_key, axis), (), 0, dims[axis]) for axis in range(len(dims))]
    entries = entries.at[tuple(place)].set(smallest)
    longest = dims.index(max(dims))
    place[longest] = (place[longest] + 1) % dims[longest]
    return entries.at[tuple(place)].set(high)


def strengthened(result, own_key, source, target, shards_of, factor):
    owner, partner = [(jnp.arange(result.shape[position]) // (result.shape[position] // shards_of)).reshape([-1 if axis == position else 1 for axis in range(result.ndim)]) for position in (source, target)]
    chosen = jax.random.permutation(own_key, shards_of)[partner]
    strong = (owner == chosen) | (owner == (partner + shards_of // 2) % shards_of)
    return jnp.where(strong, factor * result, result)


def steps_of(stream_key, dims, cuts, smallest, high):
    def one(dim, blocks):
        draws = jax.random.uniform(jax.random.fold_in(jax.random.fold_in(stream_key, 6), dim), (blocks,), jnp.float32, smallest / len(cuts), high / len(cuts))
        return jnp.repeat(jnp.exp(draws), dims[dim] // blocks).reshape((-1,) + (1,) * (len(dims) - dim - 1))

    factor_of = one(*cuts[0])
    for cut in cuts[1:]:
        factor_of = factor_of * one(*cut)
    return factor_of


def routed_block(rng, own, number, rows, amount, top, most, skew):
    ranking = jax.random.permutation(rng, amount)
    heavy_load, common = shares(amount, rows * top, most, skew, True), shares(amount, rows * top, most, skew, False)
    places = jnp.arange(amount)

    def named(tallies, offset_by):
        used = int((tallies > 0).sum())
        fixed = max(1, used // 4)
        moved = fixed + (places - fixed + offset_by * (used - fixed)) % max(1, amount - fixed)
        return jnp.zeros((amount,), jnp.int32).at[ranking[jnp.where(places < fixed, places, moved)]].set(jnp.asarray(tallies, jnp.int32))

    tallies = jnp.where(number % 4 == 0, named(heavy_load, number // 4), named(common, number - number // 4 - 1))
    mixed = jax.random.permutation(jax.random.fold_in(own, 3), amount)
    giver, taker = mixed[0:amount // 2 * 2:2], mixed[1:amount // 2 * 2:2]
    slack = jnp.minimum(tallies[giver] - 1, most - tallies[taker]) // 2
    slack = jnp.where((giver == ranking[0]) | (taker == ranking[0]) | (tallies[taker] == 0), 0, jnp.maximum(slack, 0))
    moved = jax.random.randint(jax.random.fold_in(own, 4), (amount // 2,), 0, 1 << 20) % (slack + 1)
    tallies = tallies.at[giver].add(-moved).at[taker].add(moved)
    members = jnp.searchsorted(jnp.cumsum(tallies), jnp.arange(rows * top), side="right").astype(jnp.int32)
    grid = members.reshape(top, rows).T
    grid = grid[jax.random.permutation(jax.random.fold_in(own, 1), rows)]
    offset_by = jax.random.randint(jax.random.fold_in(own, 2), (rows, 1), 0, top)
    return jnp.take_along_axis(grid, (jnp.arange(top)[None, :] + offset_by) % top, axis=1)


def shares(count, total, reach, lean, full):
    weights = [(1 << 20) // math.isqrt(standing ** lean) + 1 for standing in range(1, count + 1)]
    largest = reach if full else min(reach, max(-(-total // count), total * weights[0] // sum(weights)))
    least = 1 if total - largest >= count - 1 else 0
    counts, surplus = [largest] + [least] * (count - 1), total - largest - least * (count - 1)
    while surplus > 0:
        candidates = [i for i in range(1, count) if counts[i] < largest] or [i for i in range(1, count) if counts[i] < reach]
        whole, budget = sum([weights[i] for i in candidates]), surplus
        for i in candidates:
            addition = min(reach - counts[i], max(1, budget * weights[i] // whole), surplus)
            counts[i] = counts[i] + addition
            surplus = surplus - addition
    return np.array(counts)


def noise(key, shape, spread, bound, cuts=(), kind=jnp.bfloat16):
    drawn = spread * jax.random.normal(key, shape, jnp.float32)
    if cuts:
        drawn = drawn * steps_of(key, shape, cuts, -0.22, 0.18)
    return jnp.clip(drawn, -bound, bound).astype(kind)


def heavy_noise(stream_key, extent, spread, reach, pieces, heavy, kind=jnp.bfloat16):
    array = spread * jax.random.normal(stream_key, extent, jnp.float32)
    if pieces:
        array = array * steps_of(stream_key, extent, pieces, -0.22, 0.18)
    return jnp.clip(strengthened(array, jax.random.fold_in(stream_key, 3), *heavy), -reach, reach).astype(kind)


def setup_inputs(seed: int = 0) -> dict:
    keys = jax.random.split(jax.random.key(seed), 7)
    tokens = heavy_noise(keys[0], (TOKENS, D), 1.0, 24.0, ((0, 1024),), (0, 1, 1024, 6.0))
    upstream = noise(keys[1], (TOKENS, D), 1.0, 6.0, ((0, 1024),))
    w_up = noise(keys[2], (EXPERTS, D, F), D ** -0.5, 0.125, ((0, 64),))
    w_down = noise(keys[3], (EXPERTS, D, F), F ** -0.5, 0.21875, ((0, 64),))
    routes_keys = jax.random.split(jax.random.fold_in(keys[4], 1), TOKENS // TOK_DEV)
    routes_turns = jax.random.permutation(jax.random.fold_in(keys[4], 3), TOKENS // TOK_DEV)
    routes = jax.vmap(lambda own, number: routed_block(jax.random.fold_in(keys[4], 2), own, number, TOK_DEV, EXPERTS, TOPK, CAP, 2))(routes_keys, routes_turns).reshape((TOKENS, TOPK))
    gate_share = touch_ends(jax.random.randint(keys[5], (TOKENS, TOPK), 1, GATE_DEN + 1), jax.random.fold_in(keys[5], 1), 1, GATE_DEN).astype(jnp.int32)
    return {"tokens": tokens, "upstream": upstream, "w_up": w_up, "w_down": w_down, "routes": routes, "gate_share": gate_share}


def reference(tokens, upstream, w_up, w_down, routes, gate_share):
    token_total = tokens.shape[0]
    top_count = routes.shape[1]
    expert_total = w_up.shape[0]
    flat_routes = routes.reshape(-1).astype(jnp.int32)
    row_total = flat_routes.shape[0]
    row_ids = jnp.arange(row_total, dtype=jnp.int32)
    device_id = row_ids // (TOK_DEV * top_count)
    keyed = device_id * expert_total + flat_routes
    sort_order = jnp.argsort(keyed, stable=True).astype(jnp.int32)
    sorted_keys = keyed[sort_order]
    run_start = jnp.searchsorted(sorted_keys, sorted_keys, side="left").astype(jnp.int32)
    rank_sorted = (row_ids - run_start).astype(jnp.int32)
    slot_rank = jnp.zeros((row_total,), jnp.int32).at[sort_order].set(rank_sorted)
    data_group = device_id // N_EXPERT
    source_id = device_id % N_EXPERT
    slot_table = jnp.full((expert_total, N_DP, N_EXPERT * CAP), row_total, jnp.int32)
    slot_table = slot_table.at[flat_routes, data_group, source_id * CAP + slot_rank].set(row_ids)
    gate_values = gate_share.reshape(-1).astype(jnp.float32) / GATE_DEN

    def one_expert(carry, operands):
        grad_rows, gate_rows = carry
        slots, up_weight, down_weight = operands
        in_use = slots < row_total
        safe_rows = jnp.where(in_use, slots, 0)
        token_ids = safe_rows // top_count
        mask = in_use[..., None]
        inputs = jnp.where(mask, tokens[token_ids].astype(jnp.float32), 0.0)
        cotan = jnp.where(mask, upstream[token_ids].astype(jnp.float32), 0.0)
        gates = jnp.where(in_use, gate_values[safe_rows], 0.0)
        up_f = up_weight.astype(jnp.float32)
        down_f = down_weight.astype(jnp.float32)
        pre_act = jnp.einsum("gsd,df->gsf", inputs, up_f)
        hidden = jax.nn.silu(pre_act).astype(jnp.bfloat16)
        expert_out = jnp.einsum("gsf,df->gsd", hidden.astype(jnp.float32), down_f)
        gate_grad = jnp.sum(expert_out * cotan, axis=-1).astype(jnp.bfloat16)
        scaled = (gates[..., None] * cotan).astype(jnp.bfloat16)
        hidden_grad = jnp.einsum("gsd,df->gsf", scaled.astype(jnp.float32), down_f)
        sigmoid_a = jax.nn.sigmoid(pre_act)
        pre_grad = (hidden_grad * sigmoid_a * (1.0 + pre_act * (1.0 - sigmoid_a))).astype(jnp.bfloat16)
        row_grad = jnp.einsum("gsf,df->gsd", pre_grad.astype(jnp.float32), up_f).astype(jnp.bfloat16)
        part_up = jnp.einsum("gsd,gsf->gdf", inputs, pre_grad.astype(jnp.float32)).astype(jnp.bfloat16)
        part_up = lax.optimization_barrier(part_up)
        part_down = jnp.einsum("gsd,gsf->gdf", scaled.astype(jnp.float32), hidden.astype(jnp.float32)).astype(jnp.bfloat16)
        part_down = lax.optimization_barrier(part_down)
        up_sum = jnp.sum(part_up.astype(jnp.float32), axis=0)
        down_sum = jnp.sum(part_down.astype(jnp.float32), axis=0)
        flat_slots = slots.reshape(-1)
        grad_rows = grad_rows.at[flat_slots].set(row_grad.reshape(-1, row_grad.shape[-1]).astype(jnp.float32), mode="drop")
        gate_rows = gate_rows.at[flat_slots].set(gate_grad.reshape(-1).astype(jnp.float32), mode="drop")
        return (grad_rows, gate_rows), (up_sum, down_sum)

    start_rows = jnp.zeros((row_total, tokens.shape[1]), jnp.float32)
    start_gates = jnp.zeros((row_total,), jnp.float32)
    (grad_rows, gate_rows), (up_grad, down_grad) = lax.scan(one_expert, (start_rows, start_gates), (slot_table, w_up, w_down))
    token_grad = grad_rows.reshape(token_total, top_count, -1).sum(axis=1).astype(jnp.bfloat16)
    gate_grad = gate_rows.reshape(token_total, top_count).astype(jnp.bfloat16)
    return token_grad, gate_grad, up_grad, down_grad
```

```python
import jax
import jax.numpy as jnp
from jax import lax
from jax.experimental import pallas as pl
from jax.experimental.pallas import tpu as pltpu
from jax.sharding import PartitionSpec as P

GATE_DEN = 256
CAP = 3
LANES = 128
SIDE = 4


F32 = jnp.float32
BF16 = jnp.bfloat16
VMEM = pl.BlockSpec(memory_space=pltpu.VMEM)
SMEM = pl.BlockSpec(memory_space=pltpu.SMEM)


def columns_of(row):
    n = row.shape[1]
    return jnp.broadcast_to(row, (n, n)).T


def ranks(routes):
    n = routes.shape[1]
    here = jnp.broadcast_to(routes, (n, n))
    there = columns_of(routes)
    first = lax.broadcasted_iota(jnp.int32, (n, n), 0) < lax.broadcasted_iota(jnp.int32, (n, n), 1)
    return jnp.sum(jnp.where((here == there) & first, 1, 0), axis=0, keepdims=True)


def pack_kernel(routes_ref, gates_ref, tokens_ref, upstream_ref, out_ref, wide):
    n, features = tokens_ref.shape
    chunks = features // LANES
    slots = out_ref.shape[0] // (2 * chunks)
    routes = routes_ref[...]
    slot = routes * CAP + ranks(routes)
    pick = (lax.broadcasted_iota(jnp.int32, (slots, n), 0) == slot).astype(BF16)
    gates = columns_of(gates_ref[...].astype(F32) / GATE_DEN)
    for c in range(chunks):
        lanes = slice(c * LANES, (c + 1) * LANES)
        part = jnp.dot(pick, tokens_ref[:, lanes], preferred_element_type=F32)
        wide[pl.ds(c, slots, stride=2 * chunks), :] = part
        scaled = (gates * upstream_ref[:, lanes].astype(F32)).astype(BF16)
        part = jnp.dot(pick, scaled, preferred_element_type=F32)
        wide[pl.ds(chunks + c, slots, stride=2 * chunks), :] = part
    out_ref[...] = wide[...].astype(BF16)


def expert_kernel(
    got_ref, up_ref, down_ref, back_ref, x_ref, s_ref, hidden_ref, pre_grad_ref, wide, back_wide
):
    features = up_ref.shape[0]
    chunks = features // LANES
    rows = x_ref.shape[0]
    peers = rows // CAP
    wide[...] = got_ref[...].astype(F32)
    for r in range(CAP):
        at = slice(r * peers, (r + 1) * peers)
        for c in range(chunks):
            lanes = slice(c * LANES, (c + 1) * LANES)
            first = r * 2 * chunks + c
            x_ref[at, lanes] = wide[pl.ds(first, peers, stride=CAP * 2 * chunks), :].astype(BF16)
            first = first + chunks
            s_ref[at, lanes] = wide[pl.ds(first, peers, stride=CAP * 2 * chunks), :].astype(BF16)
    up = up_ref[...]
    pre = jnp.dot(x_ref[...], up, preferred_element_type=F32)
    hidden_grad = jnp.dot(s_ref[...], down_ref[...], preferred_element_type=F32)
    sig = jax.nn.sigmoid(pre)
    hidden = (pre * sig).astype(BF16)
    pre_grad = (hidden_grad * sig * (1.0 + pre * (1.0 - sig))).astype(BF16)
    hidden_ref[...] = hidden
    pre_grad_ref[...] = pre_grad
    dots = jnp.sum(hidden.astype(F32) * hidden_grad, axis=1, keepdims=True)
    high = dots.astype(BF16).astype(F32)
    low = dots - high
    period = back_ref.shape[0] // peers
    lane = lax.broadcasted_iota(jnp.int32, (peers, LANES), 1)
    gate = jnp.zeros((peers, LANES), F32)
    for r in range(CAP):
        at = slice(r * peers, (r + 1) * peers)
        gate = jnp.where(lane == r, high[at], gate)
        gate = jnp.where(lane == CAP + r, low[at], gate)
    for extra in range(CAP * chunks, period):
        back_wide[pl.ds(extra, peers, stride=period), :] = gate
    row_grad = lax.dot_general(pre_grad, up, (((1,), (1,)), ((), ())), preferred_element_type=F32)
    for r in range(CAP):
        for c in range(chunks):
            back_wide[pl.ds(r * chunks + c, peers, stride=period), :] = row_grad[
                r * peers : (r + 1) * peers, c * LANES : (c + 1) * LANES
            ]
    back_ref[...] = back_wide[...].astype(BF16)


def weight_kernel(at_ref, x_ref, s_ref, hidden_ref, pre_grad_ref, *outs):
    here_x, here_y = at_ref[0], at_ref[1]
    depth = x_ref.shape[1] // (SIDE * SIDE)
    turn = (((0,), (0,)), ((), ()))
    pre_grad, hidden = pre_grad_ref[...], hidden_ref[...]
    for i in range(SIDE):
        for j in range(SIDE):
            rows = slice(j * depth, (j + 1) * depth)
            owner = ((here_x + i) % SIDE) * SIDE + (here_y + j) % SIDE
            lanes = pl.ds(pl.multiple_of(owner * depth, depth), depth)
            part = lax.dot_general(x_ref[:, lanes], pre_grad, turn, preferred_element_type=F32)
            outs[i][rows, :] = part.astype(BF16)
            owner = ((here_x + j) % SIDE) * SIDE + (here_y + i) % SIDE
            lanes = pl.ds(pl.multiple_of(owner * depth, depth), depth)
            part = lax.dot_general(s_ref[:, lanes], hidden, turn, preferred_element_type=F32)
            outs[SIDE + i][rows, :] = part.astype(BF16)


def unpack_kernel(routes_ref, gates_ref, back_ref, token_ref, gate_ref, wide, rows_scratch):
    n, features = token_ref.shape
    chunks = features // LANES
    slots = rows_scratch.shape[0]
    peers = slots // CAP
    period = back_ref.shape[0] // peers
    routes = routes_ref[...]
    rank = ranks(routes)
    slot = rank * peers + routes
    pick = (lax.broadcasted_iota(jnp.int32, (slots, n), 0) == slot).astype(F32).T.astype(BF16)
    wide[...] = back_ref[...].astype(F32)
    for r in range(CAP):
        for c in range(chunks):
            rows_scratch[r * peers : (r + 1) * peers, c * LANES : (c + 1) * LANES] = wide[
                pl.ds(r * chunks + c, peers, stride=period), :
            ].astype(BF16)
    token_ref[...] = jnp.dot(pick, rows_scratch[...], preferred_element_type=F32).astype(BF16)
    gate = wide[pl.ds(CAP * chunks, peers, stride=period), :].astype(BF16)
    peer = (lax.broadcasted_iota(jnp.int32, (peers, n), 0) == routes).astype(F32).T.astype(BF16)
    mine = jnp.dot(peer, gate, preferred_element_type=F32)
    lane = lax.broadcasted_iota(jnp.int32, (n, LANES), 1)
    rank_of = columns_of(rank)
    dots = jnp.sum(jnp.where((lane == rank_of) | (lane == rank_of + CAP), mine, 0.0), axis=1, keepdims=True)
    dots = jnp.broadcast_to(dots, (n, n)).T[0:1]
    gate_ref[...] = (dots / (gates_ref[...].astype(F32) / GATE_DEN)).astype(BF16)


def shift(axis, d):
    pairs = []
    for x in range(SIDE):
        for y in range(SIDE):
            to = ((x + d) % SIDE) * SIDE + y if axis == 0 else x * SIDE + (y + d) % SIDE
            pairs.append((x * SIDE + y, to))
    return pairs


def total(parts):
    whole = parts[0].astype(F32)
    for part in parts[1:]:
        whole = whole + part.astype(F32)
    return whole


def exchange(parts, axis):
    return [parts[0]] + [lax.ppermute(parts[d], "dp", shift(axis, d)) for d in range(1, SIDE)]


def per_device(tokens, upstream, w_up, w_down, routes, gate_share):
    n, features = tokens.shape
    hidden_units = w_up.shape[2]
    peers = lax.axis_size("expert")
    slots = peers * CAP
    chunks = features // LANES
    period = CAP * chunks + 2
    routes = routes.reshape(1, n)
    gates = gate_share.reshape(1, n)
    packed = pl.pallas_call(
        pack_kernel,
        out_shape=jax.ShapeDtypeStruct((slots * 2 * chunks, LANES), BF16),
        in_specs=[VMEM] * 4,
        out_specs=VMEM,
        scratch_shapes=[pltpu.VMEM((slots * 2 * chunks, LANES), F32)],
        name="pack",
    )(routes, gates, tokens, upstream)
    got = lax.all_to_all(
        packed.reshape(peers, CAP * 2 * chunks, LANES), "expert", split_axis=0, concat_axis=0, tiled=True
    ).reshape(slots * 2 * chunks, LANES)
    back, x, s, hidden, pre_grad = pl.pallas_call(
        expert_kernel,
        out_shape=(
            jax.ShapeDtypeStruct((peers * period, LANES), BF16),
            jax.ShapeDtypeStruct((slots, features), BF16),
            jax.ShapeDtypeStruct((slots, features), BF16),
            jax.ShapeDtypeStruct((slots, hidden_units), BF16),
            jax.ShapeDtypeStruct((slots, hidden_units), BF16),
        ),
        in_specs=[VMEM] * 3,
        out_specs=(VMEM,) * 5,
        scratch_shapes=[
            pltpu.VMEM((slots * 2 * chunks, LANES), F32),
            pltpu.VMEM((peers * period, LANES), F32),
        ],
        name="expert",
    )(got, w_up[0], w_down[0])
    back = lax.all_to_all(
        back.reshape(peers * period // 2, 2, LANES), "expert", split_axis=0, concat_axis=0, tiled=True
    ).reshape(peers * period, LANES)
    here = lax.axis_index("dp")
    partials = pl.pallas_call(
        weight_kernel,
        out_shape=tuple(jax.ShapeDtypeStruct((features // SIDE, hidden_units), BF16) for _ in range(2 * SIDE)),
        in_specs=[SMEM] + [VMEM] * 4,
        out_specs=(VMEM,) * (2 * SIDE),
        name="weight",
    )(jnp.stack([here // SIDE, here % SIDE]), x, s, hidden, pre_grad)
    depth = features // (SIDE * SIDE)
    grads = []
    for which, axes in ((partials[:SIDE], (0, 1)), (partials[SIDE:], (1, 0))):
        near = exchange(which, axes[0])
        halves = [total([part[j * depth : (j + 1) * depth] for part in near]).astype(BF16) for j in range(SIDE)]
        grads.append(total(exchange(halves, axes[1]))[None])
    token_grad, gate_grad = pl.pallas_call(
        unpack_kernel,
        out_shape=(
            jax.ShapeDtypeStruct((n, features), BF16),
            jax.ShapeDtypeStruct((1, n), BF16),
        ),
        in_specs=[VMEM] * 3,
        out_specs=(VMEM,) * 2,
        scratch_shapes=[
            pltpu.VMEM((peers * period, LANES), F32),
            pltpu.VMEM((slots, features), BF16),
        ],
        name="unpack",
    )(routes, gates, back)
    return token_grad, gate_grad.reshape(n, 1), grads[0], grads[1]


def solution(mesh):
    return jax.shard_map(
        per_device,
        mesh=mesh,
        in_specs=(
            P(("dp", "expert"), None),
            P(("dp", "expert"), None),
            P("expert", None, None),
            P("expert", None, None),
            P(("dp", "expert"), None),
            P(("dp", "expert"), None),
        ),
        out_specs=(
            P(("dp", "expert"), None),
            P(("dp", "expert"), None),
            P("expert", "dp", None),
            P("expert", "dp", None),
        ),
        check_vma=False,
    )
```

```python
import jax
import jax.numpy as jnp
from jax import lax
from jax.experimental import pallas as pl
from jax.experimental.pallas import tpu as pltpu
from jax.sharding import PartitionSpec as P

GATE_DEN = 256
CAP = 3
LANES = 128
SIDE = 4


F32 = jnp.float32
BF16 = jnp.bfloat16
VMEM = pl.BlockSpec(memory_space=pltpu.VMEM)
SMEM = pl.BlockSpec(memory_space=pltpu.SMEM)


def columns_of(row):
    n = row.shape[1]
    return jnp.broadcast_to(row, (n, n)).T


def ranks(routes):
    n = routes.shape[1]
    here = jnp.broadcast_to(routes, (n, n))
    there = columns_of(routes)
    first = lax.broadcasted_iota(jnp.int32, (n, n), 0) < lax.broadcasted_iota(jnp.int32, (n, n), 1)
    return jnp.sum(jnp.where((here == there) & first, 1, 0), axis=0, keepdims=True)


def pack_kernel(routes_ref, gates_ref, tokens_ref, upstream_ref, out_ref):
    n, features = tokens_ref.shape
    slots, chunks = out_ref.shape[0], features // LANES
    routes = routes_ref[...]
    slot = routes * CAP + ranks(routes)
    pick = (lax.broadcasted_iota(jnp.int32, (slots, n), 0) == slot).astype(BF16)
    rows = jnp.dot(pick, tokens_ref[...], preferred_element_type=F32).astype(BF16)
    out_ref[:, :chunks, :] = rows.reshape(slots, chunks, LANES)
    gates = columns_of(gates_ref[...].astype(F32) / GATE_DEN)
    gates = jnp.concatenate([gates] * chunks, axis=1)
    scaled = (gates * upstream_ref[...].astype(F32)).astype(BF16)
    rows = jnp.dot(pick, scaled, preferred_element_type=F32).astype(BF16)
    out_ref[:, chunks:, :] = rows.reshape(slots, chunks, LANES)


def expert_kernel(got_ref, up_ref, down_ref, back_ref, hidden_ref, pre_grad_ref, wide, spread):
    features = up_ref.shape[0]
    slots, chunks = got_ref.shape[0], features // LANES
    peers = slots // CAP
    period = back_ref.shape[0] // peers
    up = up_ref[...]
    pre = jnp.dot(got_ref[:, :chunks, :].reshape(slots, features), up, preferred_element_type=F32)
    hidden_grad = jnp.dot(
        got_ref[:, chunks:, :].reshape(slots, features), down_ref[...], preferred_element_type=F32
    )
    sig = jax.nn.sigmoid(pre)
    hidden = (pre * sig).astype(BF16)
    pre_grad = (hidden_grad * sig * (1.0 + pre * (1.0 - sig))).astype(BF16)
    hidden_ref[...] = hidden
    pre_grad_ref[...] = pre_grad
    row_grad = lax.dot_general(pre_grad, up, (((1,), (1,)), ((), ())), preferred_element_type=F32)
    rows = row_grad.astype(BF16).reshape(slots * chunks, LANES)
    size = CAP * chunks
    for p in range(peers):
        wide[p * period : p * period + size, :] = rows[p * size : (p + 1) * size].astype(F32)
    dots = jnp.sum(hidden.astype(F32) * hidden_grad, axis=1, keepdims=True)
    spread[...] = jnp.broadcast_to(dots, (slots, LANES))
    lane = lax.broadcasted_iota(jnp.int32, (peers, LANES), 1)
    gate = jnp.zeros((peers, LANES), F32)
    for r in range(CAP):
        mine = spread[pl.ds(r, peers, stride=CAP), :]
        high = mine.astype(BF16).astype(F32)
        gate = jnp.where(lane == r, high, jnp.where(lane == CAP + r, mine - high, gate))
    for extra in range(size, period):
        wide[pl.ds(extra, peers, stride=period), :] = gate
    back_ref[...] = wide[...].astype(BF16)


def weight_kernel(at_ref, got_ref, hidden_ref, pre_grad_ref, *refs):
    *outs, x_ref, s_ref = refs
    slots, features = x_ref.shape
    chunks = features // LANES
    x_ref[...] = got_ref[:, :chunks, :].reshape(slots, features)
    s_ref[...] = got_ref[:, chunks:, :].reshape(slots, features)
    here_x, here_y = at_ref[0], at_ref[1]
    depth = x_ref.shape[1] // (SIDE * SIDE)
    turn = (((0,), (0,)), ((), ()))
    pre_grad, hidden = pre_grad_ref[...], hidden_ref[...]
    for i in range(SIDE):
        for j in range(SIDE):
            rows = slice(j * depth, (j + 1) * depth)
            owner = ((here_x + i) % SIDE) * SIDE + (here_y + j) % SIDE
            lanes = pl.ds(pl.multiple_of(owner * depth, depth), depth)
            part = lax.dot_general(x_ref[:, lanes], pre_grad, turn, preferred_element_type=F32)
            outs[i][rows, :] = part.astype(BF16)
            owner = ((here_x + j) % SIDE) * SIDE + (here_y + i) % SIDE
            lanes = pl.ds(pl.multiple_of(owner * depth, depth), depth)
            part = lax.dot_general(s_ref[:, lanes], hidden, turn, preferred_element_type=F32)
            outs[SIDE + i][rows, :] = part.astype(BF16)


def unpack_kernel(routes_ref, gates_ref, back_ref, token_ref, gate_ref, wide, packed):
    n, features = token_ref.shape
    chunks = features // LANES
    slots = packed.shape[0] // chunks
    peers = slots // CAP
    period = back_ref.shape[0] // peers
    routes = routes_ref[...]
    rank = ranks(routes)
    slot = routes * CAP + rank
    pick = (lax.broadcasted_iota(jnp.int32, (slots, n), 0) == slot).astype(F32).T.astype(BF16)
    wide[...] = back_ref[...].astype(F32)
    size = CAP * chunks
    for p in range(peers):
        packed[p * size : (p + 1) * size, :] = wide[p * period : p * period + size, :].astype(BF16)
    rows = packed[...].reshape(slots, features)
    token_ref[...] = jnp.dot(pick, rows, preferred_element_type=F32).astype(BF16)
    gate = wide[pl.ds(size, peers, stride=period), :].astype(BF16)
    peer = (lax.broadcasted_iota(jnp.int32, (peers, n), 0) == routes).astype(F32).T.astype(BF16)
    mine = jnp.dot(peer, gate, preferred_element_type=F32)
    lane = lax.broadcasted_iota(jnp.int32, (n, LANES), 1)
    rank_of = columns_of(rank)
    dots = jnp.sum(jnp.where((lane == rank_of) | (lane == rank_of + CAP), mine, 0.0), axis=1, keepdims=True)
    dots = jnp.broadcast_to(dots, (n, n)).T[0:1]
    gate_ref[...] = (dots / (gates_ref[...].astype(F32) / GATE_DEN)).astype(BF16)


def near(array):
    return pltpu.with_memory_space_constraint(array, pltpu.VMEM)


def shift(axis, d):
    pairs = []
    for x in range(SIDE):
        for y in range(SIDE):
            to = ((x + d) % SIDE) * SIDE + y if axis == 0 else x * SIDE + (y + d) % SIDE
            pairs.append((x * SIDE + y, to))
    return pairs


def total(parts):
    whole = parts[0].astype(F32)
    for part in parts[1:]:
        whole = whole + part.astype(F32)
    return whole


def exchange(parts, axis):
    return [parts[0]] + [lax.ppermute(parts[d], "dp", shift(axis, d)) for d in range(1, SIDE)]


def per_device(tokens, upstream, w_up, w_down, routes, gate_share):
    n, features = tokens.shape
    hidden_units = w_up.shape[2]
    peers = lax.axis_size("expert")
    slots = peers * CAP
    chunks = features // LANES
    period = CAP * chunks + 2
    routes = routes.reshape(1, n)
    gates = gate_share.reshape(1, n)
    packed = pl.pallas_call(
        pack_kernel,
        out_shape=jax.ShapeDtypeStruct((slots, 2 * chunks, LANES), BF16),
        in_specs=[VMEM] * 4,
        out_specs=VMEM,
        name="pack",
    )(routes, gates, tokens, upstream)
    got = lax.all_to_all(
        packed.reshape(peers, CAP * 2 * chunks, LANES), "expert", split_axis=0, concat_axis=0, tiled=True
    ).reshape(slots, 2 * chunks, LANES)
    got = near(got)
    back, hidden, pre_grad = pl.pallas_call(
        expert_kernel,
        out_shape=(
            jax.ShapeDtypeStruct((peers * period, LANES), BF16),
            jax.ShapeDtypeStruct((slots, hidden_units), BF16),
            jax.ShapeDtypeStruct((slots, hidden_units), BF16),
        ),
        in_specs=[VMEM] * 3,
        out_specs=(VMEM,) * 3,
        scratch_shapes=[pltpu.VMEM((peers * period, LANES), F32), pltpu.VMEM((slots, LANES), F32)],
        compiler_params=pltpu.CompilerParams(vmem_limit_bytes=40 << 20),
        name="expert",
    )(got, w_up[0], w_down[0])
    back = lax.all_to_all(
        back.reshape(peers * period // 2, 2, LANES), "expert", split_axis=0, concat_axis=0, tiled=True
    ).reshape(peers * period, LANES)
    back = near(back)
    here = lax.axis_index("dp")
    partials = pl.pallas_call(
        weight_kernel,
        out_shape=tuple(jax.ShapeDtypeStruct((features // SIDE, hidden_units), BF16) for _ in range(2 * SIDE)),
        in_specs=[SMEM] + [VMEM] * 3,
        out_specs=(VMEM,) * (2 * SIDE),
        scratch_shapes=[pltpu.VMEM((slots, features), BF16)] * 2,
        compiler_params=pltpu.CompilerParams(vmem_limit_bytes=32 << 20),
        name="weight",
    )(jnp.stack([here // SIDE, here % SIDE]), got, hidden, pre_grad)
    depth = features // (SIDE * SIDE)
    grads = []
    for which, axes in ((partials[:SIDE], (0, 1)), (partials[SIDE:], (1, 0))):
        parts = exchange(which, axes[0])
        halves = [total([part[j * depth : (j + 1) * depth] for part in parts]).astype(BF16) for j in range(SIDE)]
        grads.append(total(exchange(halves, axes[1]))[None])
    token_grad, gate_grad = pl.pallas_call(
        unpack_kernel,
        out_shape=(
            jax.ShapeDtypeStruct((n, features), BF16),
            jax.ShapeDtypeStruct((1, n), BF16),
        ),
        in_specs=[VMEM] * 3,
        out_specs=(VMEM,) * 2,
        scratch_shapes=[
            pltpu.VMEM((peers * period, LANES), F32),
            pltpu.VMEM((slots * chunks, LANES), BF16),
        ],
        name="unpack",
    )(routes, gates, back)
    return token_grad, gate_grad.reshape(n, 1), grads[0], grads[1]


def solution(mesh):
    return jax.shard_map(
        per_device,
        mesh=mesh,
        in_specs=(
            P(("dp", "expert"), None),
            P(("dp", "expert"), None),
            P("expert", None, None),
            P("expert", None, None),
            P(("dp", "expert"), None),
            P(("dp", "expert"), None),
        ),
        out_specs=(
            P(("dp", "expert"), None),
            P(("dp", "expert"), None),
            P("expert", "dp", None),
            P("expert", "dp", None),
        ),
        check_vma=False,
    )
```

```python
import jax
import jax.numpy as jnp
from jax import lax
from jax.experimental import pallas as pl
from jax.experimental.pallas import tpu as pltpu
from jax.sharding import PartitionSpec as P

GATE_DEN = 256
CAP = 3
LANES = 128
SIDE = 4


F32 = jnp.float32
BF16 = jnp.bfloat16
VMEM = pl.BlockSpec(memory_space=pltpu.VMEM)
SMEM = pl.BlockSpec(memory_space=pltpu.SMEM)


def columns_of(row):
    n = row.shape[1]
    return jnp.broadcast_to(row, (n, n)).T


def ranks(routes):
    n = routes.shape[1]
    here = jnp.broadcast_to(routes, (n, n))
    there = columns_of(routes)
    first = lax.broadcasted_iota(jnp.int32, (n, n), 0) < lax.broadcasted_iota(jnp.int32, (n, n), 1)
    return jnp.sum(jnp.where((here == there) & first, 1, 0), axis=0, keepdims=True)


def pack_kernel(routes_ref, gates_ref, tokens_ref, upstream_ref, out_ref):
    n, features = tokens_ref.shape
    slots, chunks = out_ref.shape[0], features // LANES
    routes = routes_ref[...]
    slot = routes * CAP + ranks(routes)
    pick = (lax.broadcasted_iota(jnp.int32, (slots, n), 0) == slot).astype(BF16)
    rows = jnp.dot(pick, tokens_ref[...], preferred_element_type=F32).astype(BF16)
    out_ref[:, :chunks, :] = rows.reshape(slots, chunks, LANES)
    gates = columns_of(gates_ref[...].astype(F32) / GATE_DEN)
    gates = jnp.concatenate([gates] * chunks, axis=1)
    scaled = (gates * upstream_ref[...].astype(F32)).astype(BF16)
    rows = jnp.dot(pick, scaled, preferred_element_type=F32).astype(BF16)
    out_ref[:, chunks:, :] = rows.reshape(slots, chunks, LANES)


def expert_kernel(
    got_ref, up_ref, down_hbm, back_ref, hidden_ref, pre_grad_ref, down_ref, s_ref, wide, spread, arrived
):
    fetch = pltpu.make_async_copy(down_hbm, down_ref, arrived)
    fetch.start()
    features = up_ref.shape[0]
    slots, chunks = got_ref.shape[0], features // LANES
    peers = slots // CAP
    period = back_ref.shape[0] // peers
    up = up_ref[...]
    pre = jnp.dot(got_ref[:, :chunks, :].reshape(slots, features), up, preferred_element_type=F32)
    s_ref[...] = got_ref[:, chunks:, :].reshape(slots, features)
    fetch.wait()
    hidden_grad = jnp.dot(s_ref[...], down_ref[...], preferred_element_type=F32)
    sig = jax.nn.sigmoid(pre)
    hidden = (pre * sig).astype(BF16)
    pre_grad = (hidden_grad * sig * (1.0 + pre * (1.0 - sig))).astype(BF16)
    hidden_ref[...] = hidden
    pre_grad_ref[...] = pre_grad
    row_grad = lax.dot_general(pre_grad, up, (((1,), (1,)), ((), ())), preferred_element_type=F32)
    rows = row_grad.astype(BF16).reshape(slots * chunks, LANES)
    size = CAP * chunks
    for p in range(peers):
        wide[p * period : p * period + size, :] = rows[p * size : (p + 1) * size].astype(F32)
    dots = jnp.sum(hidden.astype(F32) * hidden_grad, axis=1, keepdims=True)
    spread[...] = jnp.broadcast_to(dots, (slots, LANES))
    lane = lax.broadcasted_iota(jnp.int32, (peers, LANES), 1)
    gate = jnp.zeros((peers, LANES), F32)
    for r in range(CAP):
        mine = spread[pl.ds(r, peers, stride=CAP), :]
        high = mine.astype(BF16).astype(F32)
        gate = jnp.where(lane == r, high, jnp.where(lane == CAP + r, mine - high, gate))
    for extra in range(size, period):
        wide[pl.ds(extra, peers, stride=period), :] = gate
    back_ref[...] = wide[...].astype(BF16)


def weight_kernel(at_ref, got_ref, hidden_ref, pre_grad_ref, *refs):
    *outs, x_ref, s_ref = refs
    slots, features = x_ref.shape
    chunks = features // LANES
    x_ref[...] = got_ref[:, :chunks, :].reshape(slots, features)
    s_ref[...] = got_ref[:, chunks:, :].reshape(slots, features)
    here_x, here_y = at_ref[0], at_ref[1]
    depth = x_ref.shape[1] // (SIDE * SIDE)
    turn = (((0,), (0,)), ((), ()))
    pre_grad, hidden = pre_grad_ref[...], hidden_ref[...]
    for i in range(SIDE):
        for j in range(SIDE):
            rows = slice(j * depth, (j + 1) * depth)
            owner = ((here_x + i) % SIDE) * SIDE + (here_y + j) % SIDE
            lanes = pl.ds(pl.multiple_of(owner * depth, depth), depth)
            part = lax.dot_general(x_ref[:, lanes], pre_grad, turn, preferred_element_type=F32)
            outs[i][rows, :] = part.astype(BF16)
            owner = ((here_x + j) % SIDE) * SIDE + (here_y + i) % SIDE
            lanes = pl.ds(pl.multiple_of(owner * depth, depth), depth)
            part = lax.dot_general(s_ref[:, lanes], hidden, turn, preferred_element_type=F32)
            outs[SIDE + i][rows, :] = part.astype(BF16)


def unpack_kernel(routes_ref, gates_ref, back_ref, token_ref, gate_ref, wide, packed):
    n, features = token_ref.shape
    chunks = features // LANES
    slots = packed.shape[0] // chunks
    peers = slots // CAP
    period = back_ref.shape[0] // peers
    routes = routes_ref[...]
    rank = ranks(routes)
    slot = routes * CAP + rank
    pick = (lax.broadcasted_iota(jnp.int32, (slots, n), 0) == slot).astype(F32).T.astype(BF16)
    wide[...] = back_ref[...].astype(F32)
    size = CAP * chunks
    for p in range(peers):
        packed[p * size : (p + 1) * size, :] = wide[p * period : p * period + size, :].astype(BF16)
    rows = packed[...].reshape(slots, features)
    token_ref[...] = jnp.dot(pick, rows, preferred_element_type=F32).astype(BF16)
    gate = wide[pl.ds(size, peers, stride=period), :].astype(BF16)
    peer = (lax.broadcasted_iota(jnp.int32, (peers, n), 0) == routes).astype(F32).T.astype(BF16)
    mine = jnp.dot(peer, gate, preferred_element_type=F32)
    lane = lax.broadcasted_iota(jnp.int32, (n, LANES), 1)
    rank_of = columns_of(rank)
    dots = jnp.sum(jnp.where((lane == rank_of) | (lane == rank_of + CAP), mine, 0.0), axis=1, keepdims=True)
    dots = jnp.broadcast_to(dots, (n, n)).T[0:1]
    gate_ref[...] = (dots / (gates_ref[...].astype(F32) / GATE_DEN)).astype(BF16)


def near(array):
    return pltpu.with_memory_space_constraint(array, pltpu.VMEM)


def far(array):
    return pltpu.with_memory_space_constraint(array, pltpu.HBM)


def shift(axis, d):
    pairs = []
    for x in range(SIDE):
        for y in range(SIDE):
            to = ((x + d) % SIDE) * SIDE + y if axis == 0 else x * SIDE + (y + d) % SIDE
            pairs.append((x * SIDE + y, to))
    return pairs


def total(parts):
    whole = parts[0].astype(F32)
    for part in parts[1:]:
        whole = whole + part.astype(F32)
    return whole


def exchange(parts, axis):
    return [parts[0]] + [lax.ppermute(parts[d], "dp", shift(axis, d)) for d in range(1, SIDE)]


def per_device(tokens, upstream, w_up, w_down, routes, gate_share):
    n, features = tokens.shape
    hidden_units = w_up.shape[2]
    peers = lax.axis_size("expert")
    slots = peers * CAP
    chunks = features // LANES
    period = CAP * chunks + 2
    routes = routes.reshape(1, n)
    gates = gate_share.reshape(1, n)
    packed = pl.pallas_call(
        pack_kernel,
        out_shape=jax.ShapeDtypeStruct((slots, 2 * chunks, LANES), BF16),
        in_specs=[VMEM] * 4,
        out_specs=VMEM,
        compiler_params=pltpu.CompilerParams(vmem_limit_bytes=48 << 20),
        name="pack",
    )(*[far(a) for a in (routes, gates, tokens, upstream)])
    got = lax.all_to_all(
        packed.reshape(peers, CAP * 2 * chunks, LANES), "expert", split_axis=0, concat_axis=0, tiled=True
    ).reshape(slots, 2 * chunks, LANES)
    got = near(got)
    back, hidden, pre_grad = pl.pallas_call(
        expert_kernel,
        out_shape=(
            jax.ShapeDtypeStruct((peers * period, LANES), BF16),
            jax.ShapeDtypeStruct((slots, hidden_units), BF16),
            jax.ShapeDtypeStruct((slots, hidden_units), BF16),
        ),
        in_specs=[VMEM, VMEM, pl.BlockSpec(memory_space=pltpu.HBM)],
        out_specs=(VMEM,) * 3,
        scratch_shapes=[
            pltpu.VMEM(w_down.shape[1:], BF16),
            pltpu.VMEM((slots, features), BF16),
            pltpu.VMEM((peers * period, LANES), F32),
            pltpu.VMEM((slots, LANES), F32),
            pltpu.SemaphoreType.DMA,
        ],
        compiler_params=pltpu.CompilerParams(vmem_limit_bytes=40 << 20),
        name="expert",
    )(got, w_up[0], far(w_down[0]))
    back = lax.all_to_all(
        back.reshape(peers * period // 2, 2, LANES), "expert", split_axis=0, concat_axis=0, tiled=True
    ).reshape(peers * period, LANES)
    back = near(back)
    here = lax.axis_index("dp")
    partials = pl.pallas_call(
        weight_kernel,
        out_shape=tuple(jax.ShapeDtypeStruct((features // SIDE, hidden_units), BF16) for _ in range(2 * SIDE)),
        in_specs=[SMEM] + [VMEM] * 3,
        out_specs=(VMEM,) * (2 * SIDE),
        scratch_shapes=[pltpu.VMEM((slots, features), BF16)] * 2,
        compiler_params=pltpu.CompilerParams(vmem_limit_bytes=32 << 20),
        name="weight",
    )(jnp.stack([here // SIDE, here % SIDE]), got, hidden, pre_grad)
    depth = features // (SIDE * SIDE)
    grads = []
    for which, axes in ((partials[:SIDE], (0, 1)), (partials[SIDE:], (1, 0))):
        parts = exchange(which, axes[0])
        halves = [total([part[j * depth : (j + 1) * depth] for part in parts]).astype(BF16) for j in range(SIDE)]
        grads.append(total(exchange(halves, axes[1]))[None])
    token_grad, gate_grad = pl.pallas_call(
        unpack_kernel,
        out_shape=(
            jax.ShapeDtypeStruct((n, features), BF16),
            jax.ShapeDtypeStruct((1, n), BF16),
        ),
        in_specs=[VMEM] * 3,
        out_specs=(VMEM,) * 2,
        scratch_shapes=[
            pltpu.VMEM((peers * period, LANES), F32),
            pltpu.VMEM((slots * chunks, LANES), BF16),
        ],
        name="unpack",
    )(routes, gates, back)
    return token_grad, gate_grad.reshape(n, 1), grads[0], grads[1]


def solution(mesh):
    return jax.shard_map(
        per_device,
        mesh=mesh,
        in_specs=(
            P(("dp", "expert"), None),
            P(("dp", "expert"), None),
            P("expert", None, None),
            P("expert", None, None),
            P(("dp", "expert"), None),
            P(("dp", "expert"), None),
        ),
        out_specs=(
            P(("dp", "expert"), None),
            P(("dp", "expert"), None),
            P("expert", "dp", None),
            P("expert", "dp", None),
        ),
        check_vma=False,
    )
```

```python
import jax
import jax.numpy as jnp
from jax import lax
from jax.experimental import pallas as pl
from jax.experimental.pallas import tpu as pltpu
from jax.sharding import PartitionSpec as P

GATE_DEN = 256
CAP = 3
LANES = 128
SIDE = 4


F32 = jnp.float32
BF16 = jnp.bfloat16
VMEM = pl.BlockSpec(memory_space=pltpu.VMEM)
SMEM = pl.BlockSpec(memory_space=pltpu.SMEM)


def columns_of(row):
    n = row.shape[1]
    return jnp.broadcast_to(row, (n, n)).T


def ranks(routes):
    n = routes.shape[1]
    here = jnp.broadcast_to(routes, (n, n))
    there = columns_of(routes)
    first = lax.broadcasted_iota(jnp.int32, (n, n), 0) < lax.broadcasted_iota(jnp.int32, (n, n), 1)
    return jnp.sum(jnp.where((here == there) & first, 1, 0), axis=0, keepdims=True)


def pack_kernel(routes_ref, gates_ref, tokens_ref, upstream_ref, out_ref):
    n, features = tokens_ref.shape
    slots, chunks = out_ref.shape[0], features // LANES
    routes = routes_ref[...]
    slot = routes * CAP + ranks(routes)
    pick = (lax.broadcasted_iota(jnp.int32, (slots, n), 0) == slot).astype(BF16)
    rows = jnp.dot(pick, tokens_ref[...], preferred_element_type=F32).astype(BF16)
    out_ref[:, :chunks, :] = rows.reshape(slots, chunks, LANES)
    gates = columns_of(gates_ref[...].astype(F32) / GATE_DEN)
    gates = jnp.concatenate([gates] * chunks, axis=1)
    scaled = (gates * upstream_ref[...].astype(F32)).astype(BF16)
    rows = jnp.dot(pick, scaled, preferred_element_type=F32).astype(BF16)
    out_ref[:, chunks:, :] = rows.reshape(slots, chunks, LANES)


def expert_kernel(got_ref, up_ref, down_ref, back_ref, hidden_ref, pre_grad_ref, wide, spread):
    features = up_ref.shape[0]
    slots, chunks = got_ref.shape[0], features // LANES
    peers = slots // CAP
    period = back_ref.shape[0] // peers
    up = up_ref[...]
    pre = jnp.dot(got_ref[:, :chunks, :].reshape(slots, features), up, preferred_element_type=F32)
    hidden_grad = jnp.dot(
        got_ref[:, chunks:, :].reshape(slots, features), down_ref[...], preferred_element_type=F32
    )
    sig = jax.nn.sigmoid(pre)
    hidden = (pre * sig).astype(BF16)
    pre_grad = (hidden_grad * sig * (1.0 + pre * (1.0 - sig))).astype(BF16)
    hidden_ref[...] = hidden
    pre_grad_ref[...] = pre_grad
    row_grad = lax.dot_general(pre_grad, up, (((1,), (1,)), ((), ())), preferred_element_type=F32)
    rows = row_grad.astype(BF16).reshape(slots * chunks, LANES)
    size = CAP * chunks
    for p in range(peers):
        wide[p * period : p * period + size, :] = rows[p * size : (p + 1) * size].astype(F32)
    dots = jnp.sum(hidden.astype(F32) * hidden_grad, axis=1, keepdims=True)
    spread[...] = jnp.broadcast_to(dots, (slots, LANES))
    lane = lax.broadcasted_iota(jnp.int32, (peers, LANES), 1)
    gate = jnp.zeros((peers, LANES), F32)
    for r in range(CAP):
        mine = spread[pl.ds(r, peers, stride=CAP), :]
        high = mine.astype(BF16).astype(F32)
        gate = jnp.where(lane == r, high, jnp.where(lane == CAP + r, mine - high, gate))
    for extra in range(size, period):
        wide[pl.ds(extra, peers, stride=period), :] = gate
    back_ref[...] = wide[...].astype(BF16)


def weight_kernel(at_ref, got_ref, hidden_ref, pre_grad_ref, *refs):
    *outs, x_ref, s_ref = refs
    slots, features = x_ref.shape
    chunks = features // LANES
    x_ref[...] = got_ref[:, :chunks, :].reshape(slots, features)
    s_ref[...] = got_ref[:, chunks:, :].reshape(slots, features)
    here_x, here_y = at_ref[0], at_ref[1]
    depth = x_ref.shape[1] // (SIDE * SIDE)
    turn = (((0,), (0,)), ((), ()))
    pre_grad, hidden = pre_grad_ref[...], hidden_ref[...]
    for i in range(SIDE):
        for j in range(SIDE):
            rows = slice(j * depth, (j + 1) * depth)
            owner = ((here_x + i) % SIDE) * SIDE + (here_y + j) % SIDE
            lanes = pl.ds(pl.multiple_of(owner * depth, depth), depth)
            part = lax.dot_general(x_ref[:, lanes], pre_grad, turn, preferred_element_type=F32)
            outs[i][rows, :] = part.astype(BF16)
            owner = ((here_x + j) % SIDE) * SIDE + (here_y + i) % SIDE
            lanes = pl.ds(pl.multiple_of(owner * depth, depth), depth)
            part = lax.dot_general(s_ref[:, lanes], hidden, turn, preferred_element_type=F32)
            outs[SIDE + i][rows, :] = part.astype(BF16)


def unpack_kernel(routes_ref, gates_ref, back_ref, token_ref, gate_ref, wide, packed):
    n, features = token_ref.shape
    chunks = features // LANES
    slots = packed.shape[0] // chunks
    peers = slots // CAP
    period = back_ref.shape[0] // peers
    routes = routes_ref[...]
    rank = ranks(routes)
    slot = routes * CAP + rank
    pick = (lax.broadcasted_iota(jnp.int32, (slots, n), 0) == slot).astype(F32).T.astype(BF16)
    wide[...] = back_ref[...].astype(F32)
    size = CAP * chunks
    for p in range(peers):
        packed[p * size : (p + 1) * size, :] = wide[p * period : p * period + size, :].astype(BF16)
    rows = packed[...].reshape(slots, features)
    token_ref[...] = jnp.dot(pick, rows, preferred_element_type=F32).astype(BF16)
    gate = wide[pl.ds(size, peers, stride=period), :].astype(BF16)
    peer = (lax.broadcasted_iota(jnp.int32, (peers, n), 0) == routes).astype(F32).T.astype(BF16)
    mine = jnp.dot(peer, gate, preferred_element_type=F32)
    lane = lax.broadcasted_iota(jnp.int32, (n, LANES), 1)
    rank_of = columns_of(rank)
    dots = jnp.sum(jnp.where((lane == rank_of) | (lane == rank_of + CAP), mine, 0.0), axis=1, keepdims=True)
    dots = jnp.broadcast_to(dots, (n, n)).T[0:1]
    gate_ref[...] = (dots / (gates_ref[...].astype(F32) / GATE_DEN)).astype(BF16)


def near(array):
    return pltpu.with_memory_space_constraint(array, pltpu.VMEM)


def far(array):
    return pltpu.with_memory_space_constraint(array, pltpu.HBM)


def shift(axis, d):
    pairs = []
    for x in range(SIDE):
        for y in range(SIDE):
            to = ((x + d) % SIDE) * SIDE + y if axis == 0 else x * SIDE + (y + d) % SIDE
            pairs.append((x * SIDE + y, to))
    return pairs


def total(parts):
    whole = parts[0].astype(F32)
    for part in parts[1:]:
        whole = whole + part.astype(F32)
    return whole


def exchange(parts, axis):
    return [parts[0]] + [lax.ppermute(parts[d], "dp", shift(axis, d)) for d in range(1, SIDE)]


def per_device(tokens, upstream, w_up, w_down, routes, gate_share):
    n, features = tokens.shape
    hidden_units = w_up.shape[2]
    peers = lax.axis_size("expert")
    slots = peers * CAP
    chunks = features // LANES
    period = CAP * chunks + 2
    routes = routes.reshape(1, n)
    gates = gate_share.reshape(1, n)
    packed = pl.pallas_call(
        pack_kernel,
        out_shape=jax.ShapeDtypeStruct((slots, 2 * chunks, LANES), BF16),
        in_specs=[VMEM] * 4,
        out_specs=VMEM,
        compiler_params=pltpu.CompilerParams(vmem_limit_bytes=48 << 20),
        name="pack",
    )(*[far(a) for a in (routes, gates, tokens, upstream)])
    got = lax.all_to_all(
        packed.reshape(peers, CAP * 2 * chunks, LANES), "expert", split_axis=0, concat_axis=0, tiled=True
    ).reshape(slots, 2 * chunks, LANES)
    got = near(got)
    back, hidden, pre_grad = pl.pallas_call(
        expert_kernel,
        out_shape=(
            jax.ShapeDtypeStruct((peers * period, LANES), BF16),
            jax.ShapeDtypeStruct((slots, hidden_units), BF16),
            jax.ShapeDtypeStruct((slots, hidden_units), BF16),
        ),
        in_specs=[VMEM] * 3,
        out_specs=(VMEM,) * 3,
        scratch_shapes=[pltpu.VMEM((peers * period, LANES), F32), pltpu.VMEM((slots, LANES), F32)],
        compiler_params=pltpu.CompilerParams(vmem_limit_bytes=40 << 20),
        name="expert",
    )(got, w_up[0], far(w_down[0]))
    back = lax.all_to_all(
        back.reshape(peers * period // 2, 2, LANES), "expert", split_axis=0, concat_axis=0, tiled=True
    ).reshape(peers * period, LANES)
    back = near(back)
    here = lax.axis_index("dp")
    partials = pl.pallas_call(
        weight_kernel,
        out_shape=tuple(jax.ShapeDtypeStruct((features // SIDE, hidden_units), BF16) for _ in range(2 * SIDE)),
        in_specs=[SMEM] + [VMEM] * 3,
        out_specs=(VMEM,) * (2 * SIDE),
        scratch_shapes=[pltpu.VMEM((slots, features), BF16)] * 2,
        compiler_params=pltpu.CompilerParams(vmem_limit_bytes=32 << 20),
        name="weight",
    )(jnp.stack([here // SIDE, here % SIDE]), got, hidden, pre_grad)
    depth = features // (SIDE * SIDE)
    grads = []
    for which, axes in ((partials[:SIDE], (0, 1)), (partials[SIDE:], (1, 0))):
        parts = exchange(which, axes[0])
        halves = [total([part[j * depth : (j + 1) * depth] for part in parts]).astype(BF16) for j in range(SIDE)]
        grads.append(total(exchange(halves, axes[1]))[None])
    token_grad, gate_grad = pl.pallas_call(
        unpack_kernel,
        out_shape=(
            jax.ShapeDtypeStruct((n, features), BF16),
            jax.ShapeDtypeStruct((1, n), BF16),
        ),
        in_specs=[VMEM] * 3,
        out_specs=(VMEM,) * 2,
        scratch_shapes=[
            pltpu.VMEM((peers * period, LANES), F32),
            pltpu.VMEM((slots * chunks, LANES), BF16),
        ],
        name="unpack",
    )(routes, gates, back)
    return token_grad, gate_grad.reshape(n, 1), grads[0], grads[1]


def solution(mesh):
    return jax.shard_map(
        per_device,
        mesh=mesh,
        in_specs=(
            P(("dp", "expert"), None),
            P(("dp", "expert"), None),
            P("expert", None, None),
            P("expert", None, None),
            P(("dp", "expert"), None),
            P(("dp", "expert"), None),
        ),
        out_specs=(
            P(("dp", "expert"), None),
            P(("dp", "expert"), None),
            P("expert", "dp", None),
            P("expert", "dp", None),
        ),
        check_vma=False,
    )
```

```python
import jax
import jax.numpy as jnp
from jax import lax
from jax.experimental import pallas as pl
from jax.experimental.pallas import tpu as pltpu
from jax.sharding import PartitionSpec as P

GATE_DEN = 256
CAP = 3
LANES = 128
SIDE = 4


F32 = jnp.float32
BF16 = jnp.bfloat16
VMEM = pl.BlockSpec(memory_space=pltpu.VMEM)
SMEM = pl.BlockSpec(memory_space=pltpu.SMEM)


def columns_of(row):
    n = row.shape[1]
    return jnp.broadcast_to(row, (n, n)).T


def ranks(routes):
    n = routes.shape[1]
    here = jnp.broadcast_to(routes, (n, n))
    there = columns_of(routes)
    first = lax.broadcasted_iota(jnp.int32, (n, n), 0) < lax.broadcasted_iota(jnp.int32, (n, n), 1)
    return jnp.sum(jnp.where((here == there) & first, 1, 0), axis=0, keepdims=True)


def pack_kernel(routes_ref, gates_ref, tokens_ref, upstream_ref, out_ref):
    n, features = tokens_ref.shape
    slots, chunks = out_ref.shape[0], features // LANES
    routes = routes_ref[...]
    slot = routes * CAP + ranks(routes)
    pick = (lax.broadcasted_iota(jnp.int32, (slots, n), 0) == slot).astype(BF16)
    rows = jnp.dot(pick, tokens_ref[...], preferred_element_type=F32).astype(BF16)
    out_ref[:, :chunks, :] = rows.reshape(slots, chunks, LANES)
    gates = columns_of(gates_ref[...].astype(F32) / GATE_DEN)
    gates = jnp.concatenate([gates] * chunks, axis=1)
    scaled = (gates * upstream_ref[...].astype(F32)).astype(BF16)
    rows = jnp.dot(pick, scaled, preferred_element_type=F32).astype(BF16)
    out_ref[:, chunks:, :] = rows.reshape(slots, chunks, LANES)


def expert_kernel(got_ref, up_ref, down_ref, back_ref, hidden_ref, pre_grad_ref, wide, spread):
    features = up_ref.shape[0]
    slots, chunks = got_ref.shape[0], features // LANES
    peers = slots // CAP
    period = back_ref.shape[0] // peers
    up = up_ref[...]
    pre = jnp.dot(got_ref[:, :chunks, :].reshape(slots, features), up, preferred_element_type=F32)
    hidden_grad = jnp.dot(
        got_ref[:, chunks:, :].reshape(slots, features), down_ref[...], preferred_element_type=F32
    )
    sig = jax.nn.sigmoid(pre)
    hidden = (pre * sig).astype(BF16)
    pre_grad = (hidden_grad * sig * (1.0 + pre * (1.0 - sig))).astype(BF16)
    hidden_ref[...] = hidden
    pre_grad_ref[...] = pre_grad
    row_grad = lax.dot_general(pre_grad, up, (((1,), (1,)), ((), ())), preferred_element_type=F32)
    rows = row_grad.astype(BF16).reshape(slots * chunks, LANES)
    size = CAP * chunks
    for p in range(peers):
        wide[p * period : p * period + size, :] = rows[p * size : (p + 1) * size].astype(F32)
    dots = jnp.sum(hidden.astype(F32) * hidden_grad, axis=1, keepdims=True)
    spread[...] = jnp.broadcast_to(dots, (slots, LANES))
    lane = lax.broadcasted_iota(jnp.int32, (peers, LANES), 1)
    gate = jnp.zeros((peers, LANES), F32)
    for r in range(CAP):
        mine = spread[pl.ds(r, peers, stride=CAP), :]
        high = mine.astype(BF16).astype(F32)
        gate = jnp.where(lane == r, high, jnp.where(lane == CAP + r, mine - high, gate))
    for extra in range(size, period):
        wide[pl.ds(extra, peers, stride=period), :] = gate
    back_ref[...] = wide[...].astype(BF16)


def weight_kernel(at_ref, got_ref, hidden_ref, pre_grad_ref, *refs):
    *outs, x_ref, s_ref = refs
    slots, features = x_ref.shape
    chunks = features // LANES
    x_ref[...] = got_ref[:, :chunks, :].reshape(slots, features)
    s_ref[...] = got_ref[:, chunks:, :].reshape(slots, features)
    here_x, here_y = at_ref[0], at_ref[1]
    depth = x_ref.shape[1] // (SIDE * SIDE)
    turn = (((0,), (0,)), ((), ()))
    pre_grad, hidden = pre_grad_ref[...], hidden_ref[...]
    for i in range(SIDE):
        for j in range(SIDE):
            rows = slice(j * depth, (j + 1) * depth)
            owner = ((here_x + i) % SIDE) * SIDE + (here_y + j) % SIDE
            lanes = pl.ds(pl.multiple_of(owner * depth, depth), depth)
            part = lax.dot_general(x_ref[:, lanes], pre_grad, turn, preferred_element_type=F32)
            outs[i][rows, :] = part.astype(BF16)
            owner = ((here_x + j) % SIDE) * SIDE + (here_y + i) % SIDE
            lanes = pl.ds(pl.multiple_of(owner * depth, depth), depth)
            part = lax.dot_general(s_ref[:, lanes], hidden, turn, preferred_element_type=F32)
            outs[SIDE + i][rows, :] = part.astype(BF16)


def unpack_kernel(routes_ref, gates_ref, back_ref, token_ref, gate_ref, wide, packed):
    n, features = token_ref.shape
    chunks = features // LANES
    slots = packed.shape[0] // chunks
    peers = slots // CAP
    period = back_ref.shape[0] // peers
    routes = routes_ref[...]
    rank = ranks(routes)
    slot = routes * CAP + rank
    pick = (lax.broadcasted_iota(jnp.int32, (slots, n), 0) == slot).astype(F32).T.astype(BF16)
    wide[...] = back_ref[...].astype(F32)
    size = CAP * chunks
    for p in range(peers):
        packed[p * size : (p + 1) * size, :] = wide[p * period : p * period + size, :].astype(BF16)
    rows = packed[...].reshape(slots, features)
    token_ref[...] = jnp.dot(pick, rows, preferred_element_type=F32).astype(BF16)
    gate = wide[pl.ds(size, peers, stride=period), :].astype(BF16)
    peer = (lax.broadcasted_iota(jnp.int32, (peers, n), 0) == routes).astype(F32).T.astype(BF16)
    mine = jnp.dot(peer, gate, preferred_element_type=F32)
    lane = lax.broadcasted_iota(jnp.int32, (n, LANES), 1)
    rank_of = columns_of(rank)
    dots = jnp.sum(jnp.where((lane == rank_of) | (lane == rank_of + CAP), mine, 0.0), axis=1, keepdims=True)
    dots = jnp.broadcast_to(dots, (n, n)).T[0:1]
    gate_ref[...] = (dots / (gates_ref[...].astype(F32) / GATE_DEN)).astype(BF16)


def near(array):
    return pltpu.with_memory_space_constraint(array, pltpu.VMEM)


def far(array):
    return pltpu.with_memory_space_constraint(array, pltpu.HBM)


def shift(axis, d):
    pairs = []
    for x in range(SIDE):
        for y in range(SIDE):
            to = ((x + d) % SIDE) * SIDE + y if axis == 0 else x * SIDE + (y + d) % SIDE
            pairs.append((x * SIDE + y, to))
    return pairs


def total(parts):
    whole = parts[0].astype(F32)
    for part in parts[1:]:
        whole = whole + part.astype(F32)
    return whole


def exchange(parts, axis):
    return [parts[0]] + [lax.ppermute(parts[d], "dp", shift(axis, d)) for d in range(1, SIDE)]


def per_device(tokens, upstream, w_up, w_down, routes, gate_share):
    n, features = tokens.shape
    hidden_units = w_up.shape[2]
    peers = lax.axis_size("expert")
    slots = peers * CAP
    chunks = features // LANES
    period = CAP * chunks + 2
    routes = routes.reshape(1, n)
    gates = gate_share.reshape(1, n)
    packed = pl.pallas_call(
        pack_kernel,
        out_shape=jax.ShapeDtypeStruct((slots, 2 * chunks, LANES), BF16),
        in_specs=[VMEM] * 4,
        out_specs=VMEM,
        compiler_params=pltpu.CompilerParams(vmem_limit_bytes=48 << 20),
        cost_estimate=pl.CostEstimate(flops=5 * 10**9, transcendentals=0, bytes_accessed=1 << 20),
        name="pack",
    )(*[far(a) for a in (routes, gates, tokens, upstream)])
    got = lax.all_to_all(
        packed.reshape(peers, CAP * 2 * chunks, LANES), "expert", split_axis=0, concat_axis=0, tiled=True
    ).reshape(slots, 2 * chunks, LANES)
    got = near(got)
    back, hidden, pre_grad = pl.pallas_call(
        expert_kernel,
        out_shape=(
            jax.ShapeDtypeStruct((peers * period, LANES), BF16),
            jax.ShapeDtypeStruct((slots, hidden_units), BF16),
            jax.ShapeDtypeStruct((slots, hidden_units), BF16),
        ),
        in_specs=[VMEM] * 3,
        out_specs=(VMEM,) * 3,
        scratch_shapes=[pltpu.VMEM((peers * period, LANES), F32), pltpu.VMEM((slots, LANES), F32)],
        compiler_params=pltpu.CompilerParams(vmem_limit_bytes=40 << 20),
        name="expert",
    )(got, w_up[0], w_down[0])
    back = lax.all_to_all(
        back.reshape(peers * period // 2, 2, LANES), "expert", split_axis=0, concat_axis=0, tiled=True
    ).reshape(peers * period, LANES)
    back = near(back)
    here = lax.axis_index("dp")
    partials = pl.pallas_call(
        weight_kernel,
        out_shape=tuple(jax.ShapeDtypeStruct((features // SIDE, hidden_units), BF16) for _ in range(2 * SIDE)),
        in_specs=[SMEM] + [VMEM] * 3,
        out_specs=(VMEM,) * (2 * SIDE),
        scratch_shapes=[pltpu.VMEM((slots, features), BF16)] * 2,
        compiler_params=pltpu.CompilerParams(vmem_limit_bytes=32 << 20),
        name="weight",
    )(jnp.stack([here // SIDE, here % SIDE]), got, hidden, pre_grad)
    depth = features // (SIDE * SIDE)
    grads = []
    for which, axes in ((partials[:SIDE], (0, 1)), (partials[SIDE:], (1, 0))):
        parts = exchange(which, axes[0])
        halves = [total([part[j * depth : (j + 1) * depth] for part in parts]).astype(BF16) for j in range(SIDE)]
        grads.append(total(exchange(halves, axes[1]))[None])
    token_grad, gate_grad = pl.pallas_call(
        unpack_kernel,
        out_shape=(
            jax.ShapeDtypeStruct((n, features), BF16),
            jax.ShapeDtypeStruct((1, n), BF16),
        ),
        in_specs=[VMEM] * 3,
        out_specs=(VMEM,) * 2,
        scratch_shapes=[
            pltpu.VMEM((peers * period, LANES), F32),
            pltpu.VMEM((slots * chunks, LANES), BF16),
        ],
        name="unpack",
    )(routes, gates, back)
    return token_grad, gate_grad.reshape(n, 1), grads[0], grads[1]


def solution(mesh):
    return jax.shard_map(
        per_device,
        mesh=mesh,
        in_specs=(
            P(("dp", "expert"), None),
            P(("dp", "expert"), None),
            P("expert", None, None),
            P("expert", None, None),
            P(("dp", "expert"), None),
            P(("dp", "expert"), None),
        ),
        out_specs=(
            P(("dp", "expert"), None),
            P(("dp", "expert"), None),
            P("expert", "dp", None),
            P("expert", "dp", None),
        ),
        check_vma=False,
    )
```
